32 devices in a mesh: dp: 16 (over z, y, x), shard: 2 (over core).
Axes of the slice: x: 2, y: 2, z: 4, core: 2. Of those that a mesh axis runs over, the one named last changes fastest.
Arguments:
- acts: bfloat16 [4096, 2048], P('dp', 'shard'), may hold values from -6 to 6
- cotangents: bfloat16 [4096, 2048], P('dp'), may hold values from -6 to 6
- basis_old: float32 [2048, 256], P('shard'), may hold values from -0.125 to 0.125
- moment_first: float32 [2048, 256], P('shard'), may hold values from -4 to 4
- moment_second: float32 [2048, 256], P('shard'), may hold values from 0.05 to 1
Outputs:
- weight_step: float32 [2048, 2048], P('shard')
- basis_new: float32 [2048, 256], P('shard')
- first_new: float32 [2048, 256], P('shard')
- second_new: float32 [2048, 256], P('shard')
The draws below stay inside these ranges and needn't reach their ends.
All inputs are finite; a program needn't handle non-finite values.
Results may differ from the reference program's by a relative error of at most 0.0003.
Values sent between devices are 32-bit elements; how exact they have to be, the bound alone decides.
A program may use at most 64 MiB of HBM per device.

```python
import math
import jax
import jax.numpy as jnp
from jax import lax

D_IN = 2048
D_OUT = 2048
RANK = 256
NS_STEPS = 5
TOKENS = 4096


def block_scale(own_key, dims, split, least, top_value):
    gain = 1.0
    for axis_at, parts in split:
        heights = jax.random.uniform(jax.random.fold_in(jax.random.fold_in(own_key, 6), axis_at), (parts,), jnp.float32, least / len(split), top_value / len(split))
        gain = gain * jnp.repeat(jnp.exp(heights), dims[axis_at] // parts).reshape((-1,) + (1,) * (len(dims) - 1 - axis_at))
    return gain


def noise(rng, shape, spread, limit, cuts=(), dtype=jnp.bfloat16):
    result = spread * jax.random.normal(rng, shape, jnp.float32)
    if cuts:
        result = result * block_scale(rng, shape, cuts, -0.22, 0.18)
    return jnp.clip(result, -limit, limit).astype(dtype)


def setup_inputs(seed: int = 0) -> dict:
    splits = jax.random.split(jax.random.key(seed), 6)
    acts = noise(splits[0], (TOKENS, D_IN), 1.0, 6.0, ((0, 16), (1, 2)))
    cotangents = noise(splits[1], (TOKENS, D_OUT), 1.0, 6.0, ((0, 16),))
    basis_old = noise(splits[2], (D_IN, RANK), D_IN ** -0.5, 0.125, ((0, 2),), jnp.float32)
    moment_first = noise(splits[3], (D_OUT, RANK), 0.3, 4.0, ((0, 2),), jnp.float32)
    moment_second = jnp.clip(jnp.exp(math.log(1.0) - 2.9957323 * jax.random.uniform(splits[4], (D_OUT, RANK), jnp.float32) ** block_scale(splits[4], (D_OUT, RANK), ((0, 2),), -0.2, 0.2)), 0.05, 1.0)
    return dict(acts=acts, cotangents=cotangents, basis_old=basis_old, moment_first=moment_first, moment_second=moment_second)


def reference(acts, cotangents, basis_old, moment_first, moment_second):
    highest = lax.Precision.HIGHEST
    grad_t = lax.dot_general(cotangents, acts, (((0,), (0,)), ((), ())), preferred_element_type=jnp.float32)
    grad_t = grad_t * (1.0 / math.sqrt(TOKENS))
    image = jnp.dot(grad_t, basis_old, precision=highest)
    power = jnp.dot(grad_t.T, image, precision=highest)
    gram = jnp.dot(power.T, power, precision=highest)
    scale = jnp.sqrt(jnp.trace(gram))
    ortho = power / scale
    gram = gram / (scale * scale)
    for step in range(NS_STEPS):
        ortho = 1.5 * ortho - 0.5 * jnp.dot(ortho, gram, precision=highest)
        if step + 1 < NS_STEPS:
            gram = jnp.dot(ortho.T, ortho, precision=highest)
    projected = jnp.dot(grad_t, ortho, precision=highest)
    first_new = 0.9 * moment_first + 0.1 * projected
    second_new = 0.999 * moment_second + 0.001 * projected * projected
    direction = first_new / (1.0 - 0.9 ** 10) / (jnp.sqrt(second_new / (1.0 - 0.999 ** 10)) + 1e-08)
    weight_step = lax.dot_general(ortho, direction, (((1,), (1,)), ((), ())), precision=highest, preferred_element_type=jnp.float32)
    return (weight_step, ortho, first_new, second_new)
```

```python
import functools
import math

import jax
import jax.numpy as jnp
from jax import lax
from jax.experimental import pallas as pl
from jax.experimental.pallas import tpu as pltpu
from jax.sharding import PartitionSpec as P

NS_STEPS = 5
F32 = jnp.float32
BF16 = jnp.bfloat16
TILE = 256


def split(x):
    hi = x.astype(BF16)
    return hi, (x - hi.astype(F32)).astype(BF16)


def dot(a, b, dims=((1,), (0,))):
    return lax.dot_general(a, b, (dims, ((), ())), preferred_element_type=F32)


def dot3(a, b, dims=((1,), (0,))):
    a_hi, a_lo = split(a)
    b_hi, b_lo = split(b)
    return dot(a_hi, b_hi, dims) + (dot(a_hi, b_lo, dims) + dot(a_lo, b_hi, dims))


def groups(replicas):
    inner = math.gcd(replicas, 4)
    return inner, replicas // inner


def reduce_kernel(
    replicas, shards, pieces,
    acts, cot, basis, first, second,
    power, mix, q_all, first_all, second_all,
    cot_t, acts_t, part, acc, image, recv_inner, recv_outer, tok, tok_recv, gram, gram_recv, ns_g, ns_t,
    dp_send, dp_recv, sh_send, sh_recv, fwd_send, fwd_recv,
):
    inner, outer = groups(replicas)
    me = lax.axis_index("dp")
    own = lax.axis_index("shard")
    at_inner, at_outer = lax.rem(me, inner), lax.div(me, inner)
    tokens, features = acts.shape
    rows = cot.shape[1] // shards
    rank = basis.shape[1]
    width = rank // pieces
    inverse = 1.0 / math.sqrt(tokens * replicas)

    def dp_inner(k):
        return at_outer * inner + lax.rem(at_inner + k, inner)

    def dp_outer(k):
        return lax.rem(at_outer + k, outer) * inner + at_inner

    def remote(src, dst, send, recv, where):
        copy = pltpu.make_async_remote_copy(
            src_ref=src, dst_ref=dst, send_sem=send, recv_sem=recv,
            device_id=where, device_id_type=pl.DeviceIdType.MESH,
        )
        copy.start()
        return copy

    def to_shard(k):
        return (me, lax.rem(own + k, shards))

    barrier = pltpu.get_barrier_semaphore()
    for k in range(1, inner):
        pl.semaphore_signal(barrier, inc=1, device_id=(dp_inner(k), own), device_id_type=pl.DeviceIdType.MESH)
    for k in range(1, outer):
        pl.semaphore_signal(barrier, inc=1, device_id=(dp_outer(k), own), device_id_type=pl.DeviceIdType.MESH)
    for k in range(1, shards):
        pl.semaphore_signal(barrier, inc=1, device_id=to_shard(k), device_id_type=pl.DeviceIdType.MESH)

    def tiles(count, fn):
        step = min(TILE, count)

        def one(i, carry):
            fn(pl.multiple_of(i * step, step), step)
            return carry

        lax.fori_loop(0, count // step, one, 0)

    def transposes(at, n):
        cot_t[pl.ds(at, n), :] = cot[:, pl.ds(pl.multiple_of(own * rows + at, 128), n)].T

    def transposes_acts(at, n):
        acts_t[pl.ds(at, n), :] = acts[:, pl.ds(at, n)].T

    def read(ref, count, at, n):
        return jnp.concatenate([ref[pl.ds(s * count + at, n), :] for s in range(pieces)], axis=1)

    def contract(left, column, ref, count, out):
        out[...] = jnp.zeros_like(out)

        def one(at, n):
            hi, lo = split(read(ref, count, at, n))
            block = left[:, pl.ds(pl.multiple_of(column + at, 128), n)]
            out[...] += dot(block, hi) + dot(block, lo)

        tiles(count, one)

    def expand(left, right, count):
        hi, lo = split(right)

        def one(at, n):
            block = left[pl.ds(at, n), :]
            value = dot(block, hi) + dot(block, lo)
            for s in range(pieces):
                part[pl.ds(s * count + at, n), :] = value[:, s * width : (s + 1) * width]

        tiles(count, one)

    def exchange(index, buffer, received):
        return [
            remote(buffer, received.at[k - 1], sh_send.at[index, k - 1], sh_recv.at[index, k - 1], to_shard(k))
            for k in range(1, shards)
        ]

    def total(copies, buffer, received):
        value = buffer[...]
        for k, copy in enumerate(copies):
            copy.wait()
            value = value + received[k]
        return value

    def reduce_start(index, count):
        chunk = count * pieces // inner
        copies = []
        for k in range(1, inner):
            at = pl.multiple_of(lax.rem(at_inner + k, inner) * chunk, 8)
            copies.append(remote(
                part.at[pl.ds(at, chunk), :], recv_inner.at[index, k - 1],
                dp_send.at[index, 0, k - 1], dp_recv.at[index, 0, k - 1], (dp_inner(k), own),
            ))
        return copies

    def reduce_finish(index, count, full, copies, arrived=None):
        chunk = count * pieces // inner
        small = chunk // outer
        base = pl.multiple_of(at_inner * chunk, 8)
        for copy in copies:
            copy.wait()
        value = part[pl.ds(base, chunk), :]
        for k in range(1, inner):
            value = value + recv_inner[index, k - 1]
        acc[...] = value
        copies = []
        for k in range(1, outer):
            at = pl.multiple_of(lax.rem(at_outer + k, outer) * small, 8)
            copies.append(remote(
                acc.at[pl.ds(at, small), :], recv_outer.at[index, k - 1],
                dp_send.at[index, 1, k - 1], dp_recv.at[index, 1, k - 1], (dp_outer(k), own),
            ))
        for copy in copies:
            copy.wait()
        value = acc[pl.ds(pl.multiple_of(at_outer * small, 8), small), :]
        for k in range(1, outer):
            value = value + recv_outer[index, k - 1]
        mine = pl.ds(pl.multiple_of(base + at_outer * small, 8), small)
        full[mine, :] = value
        copies = [
            remote(
                full.at[mine, :], full.at[mine, :],
                dp_send.at[index, 2, k - 1], dp_recv.at[index, 2, k - 1], (dp_outer(k), own),
            )
            for k in range(1, outer)
        ]
        for copy in copies:
            copy.wait()
        mine = pl.ds(base, chunk)
        copies = [
            remote(
                full.at[mine, :], full.at[mine, :],
                dp_send.at[index, 3, k - 1], dp_recv.at[index, 3, k - 1], (dp_inner(k), own),
            )
            for k in range(1, inner)
        ]
        forwards = []
        if arrived is not None:
            forwards += arrived(0, base, chunk)
        for k, copy in enumerate(copies):
            copy.wait_recv()
            if arrived is not None:
                at = pl.multiple_of(lax.rem(at_inner + inner - k - 1, inner) * chunk, 8)
                forwards += arrived(k + 1, at, chunk)
        for copy in copies:
            copy.wait_send()
        for copy in forwards:
            copy.wait()

    contract(acts, 0, basis, features, tok.at[0]) if pieces == 1 else None
    if pieces > 1:
        tok[0] = jnp.zeros_like(tok[0])

        def one(at, n):
            hi, lo = split(basis[pl.ds(at, n), :])
            block = acts[:, pl.ds(at, n)]
            tok[0] += dot(block, hi) + dot(block, lo)

        tiles(features, one)
    pl.semaphore_wait(barrier, inner + outer + shards - 3)
    copies = exchange(0, tok.at[0], tok_recv.at[0])
    moments = []
    for k in range(1, shards):
        slot = pl.ds((shards - k) * rows, rows)
        moments.append(remote(
            first, first_all.at[slot, :], sh_send.at[4, k - 1], sh_recv.at[4, k - 1], to_shard(k)))
        moments.append(remote(
            second, second_all.at[slot, :], sh_send.at[5, k - 1], sh_recv.at[5, k - 1], to_shard(k)))
    first_all[pl.ds(0, rows), :] = first[...]
    second_all[pl.ds(0, rows), :] = second[...]
    tiles(rows, transposes)
    value = total(copies, tok.at[0], tok_recv.at[0]) * inverse
    expand(cot_t, value, rows)
    copies = reduce_start(0, rows)
    tiles(features, transposes_acts)
    reduce_finish(0, rows, image, copies)

    contract(cot, own * rows, image, rows, tok.at[1])
    copies = exchange(1, tok.at[1], tok_recv.at[1])
    value = total(copies, tok.at[1], tok_recv.at[1]) * inverse
    expand(acts_t, value, features)
    copies = reduce_start(1, features)
    reduce_finish(1, features, power, copies)

    contract(acts, 0, power, features, tok.at[2])
    copies = exchange(2, tok.at[2], tok_recv.at[2])
    gram[...] = jnp.zeros_like(gram)

    def one_gram(at, n):
        hi, lo = split(read(power, features, at, n))
        hi_t = hi.T
        cross = dot(hi_t, lo)
        gram[...] += dot(hi_t, hi) + (cross + cross.T)

    tiles(features, one_gram)
    gram_copies = exchange(3, gram, gram_recv)
    value = total(copies, tok.at[2], tok_recv.at[2]) * inverse
    expand(cot_t, value, rows)
    copies = reduce_start(2, rows)

    g = total(gram_copies, gram, gram_recv)
    diagonal = lax.broadcasted_iota(jnp.int32, g.shape, 0) == lax.broadcasted_iota(jnp.int32, g.shape, 1)
    identity = jnp.where(diagonal, 1.0, 0.0).astype(F32)
    scale = jnp.sqrt(jnp.sum(jnp.where(diagonal, g, 0.0), keepdims=True))
    g = g / (scale * scale)
    ns_g[...] = g
    ns_t[...] = 1.5 * identity - 0.5 * g

    def newton(i, carry):
        g = ns_g[...]
        factor = 1.5 * identity - 0.5 * g
        g = dot3(dot3(g, factor), factor)
        ns_g[...] = g
        ns_t[...] = dot3(ns_t[...], 1.5 * identity - 0.5 * g)
        return carry

    lax.fori_loop(0, NS_STEPS - 1, newton, 0)
    mix[...] = ns_t[...] / scale

    def arrived(j, at, n):
        return [
            remote(
                q_all.at[pl.ds(at, n), :],
                q_all.at[pl.ds(pl.multiple_of((shards - k) * rows * pieces + at, 8), n), :],
                fwd_send.at[j, k - 1], fwd_recv.at[j, k - 1], to_shard(k),
            )
            for k in range(1, shards)
        ]

    reduce_finish(2, rows, q_all, copies, arrived)
    for copy in moments:
        copy.wait()


def finish_kernel(blocks, where, power, mix, q, first, second, step_out, basis_out, first_out, second_out, right):
    j = pl.program_id(0)

    @pl.when(j == 0)
    def _():
        count = power.shape[0]
        tile = min(TILE, count)
        for i in range(count // tile):
            at = pl.ds(i * tile, tile)
            basis_out[at, :] = dot3(power[at, :], mix[...])

    projected = dot3(q[...], mix[...])
    first_new = 0.9 * first[...] + 0.1 * projected
    second_new = 0.999 * second[...] + 0.001 * projected * projected

    @pl.when(j < blocks)
    def _():
        first_out[...] = first_new
        second_out[...] = second_new

    direction = first_new / (1.0 - 0.9**10) / (jnp.sqrt(second_new / (1.0 - 0.999**10)) + 1e-08)
    right[...] = direction.T
    hi, lo = split(right[...])
    count = power.shape[0]
    tile = min(TILE, count)
    for i in range(count // tile):
        at = pl.ds(i * tile, tile)
        a_hi, a_lo = split(basis_out[at, :])
        step_out[at, :] = dot(a_hi, hi) + (dot(a_hi, lo) + dot(a_lo, hi))


def body(replicas, shards, acts, cotangents, basis_old, moment_first, moment_second):
    tokens, features = acts.shape
    outs = cotangents.shape[1]
    rows = outs // shards
    rank = basis_old.shape[1]
    inner, outer = groups(replicas)
    pieces = 1 if min(rows, features) // replicas % 8 == 0 else 2
    width = rank // pieces
    most = max(rows, features) * pieces
    vmem = pl.BlockSpec(memory_space=pltpu.VMEM)
    links = max(inner, outer)
    sem = pltpu.SemaphoreType.DMA
    power, mix, q_all, first_all, second_all = pl.pallas_call(
        functools.partial(reduce_kernel, replicas, shards, pieces),
        out_shape=[
            jax.ShapeDtypeStruct((features * pieces, width), F32),
            jax.ShapeDtypeStruct((rank, rank), F32),
            jax.ShapeDtypeStruct((outs * pieces, width), F32),
            jax.ShapeDtypeStruct((outs, rank), F32),
            jax.ShapeDtypeStruct((outs, rank), F32),
        ],
        in_specs=[vmem] * 5,
        out_specs=[vmem] * 5,
        scratch_shapes=[
            pltpu.VMEM((rows, tokens), BF16),
            pltpu.VMEM((features, tokens), BF16),
            pltpu.VMEM((most, width), F32),
            pltpu.VMEM((most // inner, width), F32),
            pltpu.VMEM((rows * pieces, width), F32),
            pltpu.VMEM((3, inner - 1, most // inner, width), F32),
            pltpu.VMEM((3, outer - 1, most // inner // outer, width), F32),
            pltpu.VMEM((3, tokens, rank), F32),
            pltpu.VMEM((3, shards - 1, tokens, rank), F32),
            pltpu.VMEM((rank, rank), F32),
            pltpu.VMEM((shards - 1, rank, rank), F32),
            pltpu.VMEM((rank, rank), F32),
            pltpu.VMEM((rank, rank), F32),
            sem((3, 4, links)),
            sem((3, 4, links)),
            sem((6, shards)),
            sem((6, shards)),
            sem((inner, shards)),
            sem((inner, shards)),
        ],
        compiler_params=pltpu.CompilerParams(
            collective_id=0, has_side_effects=True, vmem_limit_bytes=48 * 2**20
        ),
    )(acts, cotangents, basis_old, moment_first, moment_second)
    if pieces > 1:
        power = power.reshape(pieces, features, width).transpose(1, 0, 2).reshape(features, rank)
        q_all = q_all.reshape(shards, pieces, rows, width).transpose(0, 2, 1, 3).reshape(outs, rank)

    tile = min(TILE, rows)
    blocks = rows // tile
    where = lax.axis_index("shard").astype(jnp.int32).reshape(1)

    def column(j, at):
        return (0, lax.rem(at[0] + lax.div(j, blocks), shards) * blocks + lax.rem(j, blocks))

    fixed = lambda j, at: (0, 0)
    along = lambda j, at: (j, 0)
    early = lambda j, at: (jnp.minimum(j, blocks - 1), 0)
    return pl.pallas_call(
        functools.partial(finish_kernel, blocks),
        out_shape=[
            jax.ShapeDtypeStruct((features, outs), F32),
            jax.ShapeDtypeStruct((features, rank), F32),
            jax.ShapeDtypeStruct((rows, rank), F32),
            jax.ShapeDtypeStruct((rows, rank), F32),
        ],
        grid_spec=pltpu.PrefetchScalarGridSpec(
            num_scalar_prefetch=1,
            grid=(outs // tile,),
            in_specs=[
                pl.BlockSpec((features, rank), fixed),
                pl.BlockSpec((rank, rank), fixed),
                pl.BlockSpec((tile, rank), along),
                pl.BlockSpec((tile, rank), along),
                pl.BlockSpec((tile, rank), along),
            ],
            out_specs=[
                pl.BlockSpec((features, tile), column),
                pl.BlockSpec((features, rank), fixed),
                pl.BlockSpec((tile, rank), early),
                pl.BlockSpec((tile, rank), early),
            ],
            scratch_shapes=[pltpu.VMEM((rank, tile), F32)],
        ),
        compiler_params=pltpu.CompilerParams(vmem_limit_bytes=48 * 2**20),
    )(where, power, mix, q_all, first_all, second_all)


def solution(mesh):
    placed = (P("dp", "shard"), P("dp", None), P("shard", None), P("shard", None), P("shard", None))
    return jax.shard_map(
        functools.partial(body, mesh.shape["dp"], mesh.shape["shard"]),
        mesh=mesh,
        in_specs=placed,
        out_specs=(P("shard", None), P("shard", None), P("shard", None), P("shard", None)),
        check_vma=False,
    )
```

```python
import functools
import math

import jax
import jax.numpy as jnp
from jax import lax
from jax.experimental import pallas as pl
from jax.experimental.pallas import tpu as pltpu
from jax.sharding import PartitionSpec as P

NS_STEPS = 5
F32 = jnp.float32
BF16 = jnp.bfloat16
TILE = 256
BLOCKS = 4
WHOLE_VMEM = 62 * 2**20


def split(x):
    hi = x.astype(BF16)
    return hi, (x - hi.astype(F32)).astype(BF16)


def dot(a, b, dims=((1,), (0,))):
    return lax.dot_general(a, b, (dims, ((), ())), preferred_element_type=F32)


def dot3(a, b, dims=((1,), (0,))):
    a_hi, a_lo = split(a)
    b_hi, b_lo = split(b)
    return dot(a_hi, b_hi, dims) + (dot(a_hi, b_lo, dims) + dot(a_lo, b_hi, dims))


def stages(replicas, odd):
    pairs, stride, left = [], 1, replicas
    while left % 2 == 0 and len(pairs) < 2:
        pairs.append((stride, 2))
        stride, left = stride * 2, left // 2
    if odd:
        pairs = pairs[::-1]
    return pairs + [(stride, left)]


def reduce_kernel(
    replicas, shards, pieces, blocks,
    acts_in, cot_in, basis_in, first, second,
    power, mix, q_all, first_all, second_all,
    acts, cot, basis, cot_t, acts_t, part, image, recv_a, recv_b, recv_c, tok, tok_recv, gram, gram_recv, ns_g, ns_t,
    load_sem, dp_send, dp_recv, sh_send, sh_recv, fwd_send, fwd_recv,
):
    me = lax.axis_index("dp")
    own = lax.axis_index("shard")
    tokens, features = acts.shape
    rows = cot.shape[1] // shards
    rank = basis.shape[1]
    width = rank // pieces
    inverse = 1.0 / math.sqrt(tokens * replicas)
    receive = (recv_a, recv_b, recv_c)
    mesh_id = pl.DeviceIdType.MESH

    loads = [
        pltpu.make_async_copy(basis_in, basis, load_sem.at[0]),
        pltpu.make_async_copy(acts_in, acts, load_sem.at[1]),
        pltpu.make_async_copy(cot_in, cot, load_sem.at[2]),
    ]
    for load in loads:
        load.start()

    def place(stride, size):
        return lax.rem(lax.div(me, stride), size)

    def peer(stride, size, k):
        at = place(stride, size)
        return me + (lax.rem(at + k, size) - at) * stride

    def remote(src, dst, send, recv, where):
        copy = pltpu.make_async_remote_copy(
            src_ref=src, dst_ref=dst, send_sem=send, recv_sem=recv,
            device_id=where, device_id_type=mesh_id,
        )
        copy.start()
        return copy

    def to_shard(k):
        return (me, lax.rem(own + k, shards))

    barrier = pltpu.get_barrier_semaphore()
    greeted = 0
    for stride, size in stages(replicas, False):
        for k in range(1, size):
            pl.semaphore_signal(barrier, inc=1, device_id=(peer(stride, size, k), own), device_id_type=mesh_id)
            greeted += 1
    for k in range(1, shards):
        pl.semaphore_signal(barrier, inc=1, device_id=to_shard(k), device_id_type=mesh_id)
        greeted += 1

    def tiles(start, count, fn):
        step = min(TILE, count)
        if count == step:
            fn(start, step)
            return

        def one(i, carry):
            fn(pl.multiple_of(start + i * step, step), step)
            return carry

        lax.fori_loop(0, count // step, one, 0)

    def turn_cot(at, n):
        cot_t[pl.ds(at, n), :] = cot[:, pl.ds(pl.multiple_of(own * rows + at, 128), n)].T

    def turn_acts(at, n):
        acts_t[pl.ds(at, n), :] = acts[:, pl.ds(at, n)].T

    def read(ref, count, at, n):
        if pieces == 1:
            return ref[pl.ds(at, n), :]
        return jnp.concatenate([ref[pl.ds(s * count + at, n), :] for s in range(pieces)], axis=1)

    def contract(left, column, hi, lo, at, n, out, fresh):
        block = left[:, pl.ds(pl.multiple_of(column + at, 128), n)]
        value = dot(block, hi) + dot(block, lo)
        if fresh:
            out[...] = value
        else:
            out[...] += value

    def exchange(index, buffer, received):
        return [
            remote(buffer, received.at[k - 1], sh_send.at[index, k - 1], sh_recv.at[index, k - 1], to_shard(k))
            for k in range(1, shards)
        ]

    def total(copies, buffer, received):
        value = buffer[...]
        for k, copy in enumerate(copies):
            copy.wait()
            value = value + received[k]
        return value

    def piece(index, h, count, left, hi, lo, full, consume):
        length = count * pieces // blocks
        base = h * length

        def expand(at, n):
            block = left[pl.ds(at, n), :]
            value = dot(block, hi) + dot(block, lo)
            for s in range(pieces):
                part[pl.ds(s * count + at, n), :] = value[:, s * width : (s + 1) * width]

        tiles(h * (count // blocks), count // blocks, expand)
        slot = index * blocks + h
        path = stages(replicas, h % 2 == 1)
        for stage, (stride, size) in enumerate(path):
            chunk = length // size
            at = place(stride, size)
            copies = [
                remote(
                    part.at[pl.ds(pl.multiple_of(base + lax.rem(at + k, size) * chunk, 8), chunk), :],
                    receive[stage].at[slot, k - 1],
                    dp_send.at[slot, stage, k - 1], dp_recv.at[slot, stage, k - 1], (peer(stride, size, k), own),
                )
                for k in range(1, size)
            ]
            yield
            base = pl.multiple_of(base + at * chunk, 8)
            length = chunk
            value = part[pl.ds(base, chunk), :]
            for k, copy in enumerate(copies):
                copy.wait()
                value = value + receive[stage][slot, k]
            if stage + 1 < len(path):
                part[pl.ds(base, chunk), :] = value
            else:
                full[pl.ds(base, chunk), :] = value
        for stage, (stride, size) in reversed(list(enumerate(path))):
            mine = full.at[pl.ds(base, length), :]
            copies = [
                remote(
                    mine, mine,
                    dp_send.at[slot, 3 + stage, k - 1], dp_recv.at[slot, 3 + stage, k - 1], (peer(stride, size, k), own),
                )
                for k in range(1, size)
            ]
            yield
            for copy in copies:
                copy.wait()
            base = pl.multiple_of(base - place(stride, size) * length, 8)
            length = length * size
        consume(h)

    def run(index, count, left, value, full, consume, beside=None):
        hi, lo = split(value)
        active = []
        for h in range(blocks):
            active.append(piece(index, h, count, left, hi, lo, full, consume))
            next(active[h])
        if beside is not None:
            active.append(beside())
        while active:
            active = [one for one in active if next(one, one) is None]

    loads[0].wait()
    loads[1].wait()

    def project(at, n):
        hi, lo = split(basis[pl.ds(at, n), :])
        block = acts[:, pl.ds(at, n)]
        tok[0] += dot(block, hi) + dot(block, lo)

    tok[0] = jnp.zeros_like(tok[0])
    tiles(0, features, project)
    loads[2].wait()
    pl.semaphore_wait(barrier, greeted)
    copies = exchange(0, tok.at[0], tok_recv.at[0])
    tiles(0, rows, turn_cot)
    value = total(copies, tok.at[0], tok_recv.at[0]) * inverse
    moments = []

    def early():
        for k in range(1, shards):
            slot = pl.ds((shards - k - 1) * rows, rows)
            moments.append(remote(
                first, first_all.at[slot, :], sh_send.at[4, k - 1], sh_recv.at[4, k - 1], to_shard(k)))
            moments.append(remote(
                second, second_all.at[slot, :], sh_send.at[5, k - 1], sh_recv.at[5, k - 1], to_shard(k)))
        tiles(0, features, turn_acts)
        yield

    def use_image(h):
        def one(at, n):
            hi, lo = split(read(image, rows, at, n))
            contract(cot, own * rows, hi, lo, at, n, tok.at[1], h == 0)

        tiles(h * (rows // blocks), rows // blocks, one)

    run(0, rows, cot_t, value, image, use_image, early)
    copies = exchange(1, tok.at[1], tok_recv.at[1])
    value = total(copies, tok.at[1], tok_recv.at[1]) * inverse

    def use_power(h):
        def one(at, n):
            hi, lo = split(read(power, features, at, n))
            contract(acts, 0, hi, lo, at, n, tok.at[2], h == 0)
            hi_t = hi.T
            cross = dot(hi_t, lo)
            value = dot(hi_t, hi) + (cross + cross.T)
            if h == 0:
                gram[...] = value
            else:
                gram[...] += value

        tiles(h * (features // blocks), features // blocks, one)

    run(1, features, acts_t, value, power, use_power)
    copies = exchange(2, tok.at[2], tok_recv.at[2])
    gram_copies = exchange(3, gram, gram_recv)
    value = total(copies, tok.at[2], tok_recv.at[2]) * inverse

    def newton():
        g = total(gram_copies, gram, gram_recv)
        diagonal = lax.broadcasted_iota(jnp.int32, g.shape, 0) == lax.broadcasted_iota(jnp.int32, g.shape, 1)
        scale = jnp.sqrt(jnp.sum(jnp.where(diagonal, g, 0.0), keepdims=True))
        g = g / (scale * scale)

        def factor_of(g):
            return jnp.where(diagonal, 1.5, 0.0) - 0.5 * g

        ns_g[...] = g
        ns_t[...] = factor_of(g)
        yield
        for _ in range(NS_STEPS - 1):
            factor = factor_of(ns_g[...])
            g = dot3(dot3(ns_g[...], factor), factor)
            ns_g[...] = g
            ns_t[...] = dot3(ns_t[...], factor_of(g))
            yield
        mix[...] = ns_t[...] / scale

    forwards = []

    def pass_on(h):
        n = rows * pieces // blocks
        at = h * n
        for k in range(1, shards):
            forwards.append(remote(
                q_all.at[pl.ds(at, n), :],
                q_all.at[pl.ds((shards - k) * rows * pieces + at, n), :],
                fwd_send.at[h, k - 1], fwd_recv.at[h, k - 1], to_shard(k),
            ))

    run(2, rows, cot_t, value, q_all, pass_on, newton)
    for copy in moments + forwards:
        copy.wait()


def finish_kernel(
    blocks, where, power, mix, q, first, second, first_far, second_far,
    step_out, basis_out, first_out, second_out, basis_hi, basis_lo, mean, square,
):
    j = pl.program_id(0)
    count = power.shape[0]
    tile = min(TILE, count)

    @pl.when(j == 0)
    def _():
        for i in range(count // tile):
            at = pl.ds(i * tile, tile)
            value = dot3(power[at, :], mix[...])
            basis_out[at, :] = value
            hi, lo = split(value)
            basis_hi[at, :] = hi
            basis_lo[at, :] = lo

    projected = dot3(q[...], mix[...])

    def adam(first, second):
        mean[...] = 0.9 * first[...] + 0.1 * projected
        square[...] = 0.999 * second[...] + 0.001 * projected * projected

    @pl.when(j < blocks)
    def _():
        adam(first, second)
        first_out[...] = mean[...]
        second_out[...] = square[...]

    @pl.when(j >= blocks)
    def _():
        adam(first_far, second_far)

    direction = mean[...] / (1.0 - 0.9**10) / (jnp.sqrt(square[...] / (1.0 - 0.999**10)) + 1e-08)
    hi, lo = split(direction)
    hi, lo = hi.T, lo.T
    for i in range(count // tile):
        at = pl.ds(i * tile, tile)
        a_hi = basis_hi[at, :]
        step_out[at, :] = dot(a_hi, hi) + (dot(a_hi, lo) + dot(basis_lo[at, :], hi))


def body(replicas, shards, acts, cotangents, basis_old, moment_first, moment_second):
    tokens, features = acts.shape
    outs = cotangents.shape[1]
    rows = outs // shards
    rank = basis_old.shape[1]
    least = min(rows, features)
    pieces = 1 if least // replicas % 8 == 0 else 2
    blocks = BLOCKS
    while blocks > 1 and least * pieces // (replicas * blocks) % 8:
        blocks //= 2
    width = rank // pieces
    most = max(rows, features) * pieces
    vmem = pl.BlockSpec(memory_space=pltpu.VMEM)
    hbm = pl.BlockSpec(memory_space=pltpu.HBM)
    sizes = [size for _, size in stages(replicas, False)]
    links = max(sizes)
    slots = 3 * blocks
    sem = pltpu.SemaphoreType.DMA
    receive, length = [], most // blocks
    for size in sizes:
        length //= size
        receive.append(pltpu.VMEM((slots, max(size - 1, 1), length, width), F32))
    far = (max(shards - 1, 1) * rows, rank)
    power, mix, q_all, first_all, second_all = pl.pallas_call(
        functools.partial(reduce_kernel, replicas, shards, pieces, blocks),
        out_shape=[
            jax.ShapeDtypeStruct((features * pieces, width), F32),
            jax.ShapeDtypeStruct((rank, rank), F32),
            jax.ShapeDtypeStruct((outs * pieces, width), F32),
            jax.ShapeDtypeStruct(far, F32),
            jax.ShapeDtypeStruct(far, F32),
        ],
        in_specs=[hbm] * 5,
        out_specs=[vmem] * 3 + [hbm] * 2,
        scratch_shapes=[
            pltpu.VMEM((tokens, features), BF16),
            pltpu.VMEM((tokens, outs), BF16),
            pltpu.VMEM((features, rank), F32),
            pltpu.VMEM((rows, tokens), BF16),
            pltpu.VMEM((features, tokens), BF16),
            pltpu.VMEM((most, width), F32),
            pltpu.VMEM((rows * pieces, width), F32),
            *receive,
            pltpu.VMEM((3, tokens, rank), F32),
            pltpu.VMEM((3, shards - 1, tokens, rank), F32),
            pltpu.VMEM((rank, rank), F32),
            pltpu.VMEM((shards - 1, rank, rank), F32),
            pltpu.VMEM((rank, rank), F32),
            pltpu.VMEM((rank, rank), F32),
            sem((3,)),
            sem((slots, 6, links)),
            sem((slots, 6, links)),
            sem((6, shards)),
            sem((6, shards)),
            sem((blocks, shards)),
            sem((blocks, shards)),
        ],
        compiler_params=pltpu.CompilerParams(
            collective_id=0, has_side_effects=True, vmem_limit_bytes=WHOLE_VMEM
        ),
    )(acts, cotangents, basis_old, moment_first, moment_second)
    if pieces > 1:
        power = power.reshape(pieces, features, width).transpose(1, 0, 2).reshape(features, rank)
        q_all = q_all.reshape(shards, pieces, rows, width).transpose(0, 2, 1, 3).reshape(outs, rank)

    tile = min(TILE, rows)
    blocks = rows // tile
    where = lax.axis_index("shard").astype(jnp.int32).reshape(1)

    def column(j, at):
        return (0, lax.rem(at[0] + lax.div(j, blocks), shards) * blocks + lax.rem(j, blocks))

    fixed = lambda j, at: (0, 0)
    along = lambda j, at: (j, 0)
    early = lambda j, at: (jnp.minimum(j, blocks - 1), 0)
    late = lambda j, at: (jnp.maximum(j - blocks, 0), 0)
    return pl.pallas_call(
        functools.partial(finish_kernel, blocks),
        out_shape=[
            jax.ShapeDtypeStruct((features, outs), F32),
            jax.ShapeDtypeStruct((features, rank), F32),
            jax.ShapeDtypeStruct((rows, rank), F32),
            jax.ShapeDtypeStruct((rows, rank), F32),
        ],
        grid_spec=pltpu.PrefetchScalarGridSpec(
            num_scalar_prefetch=1,
            grid=(outs // tile,),
            in_specs=[
                pl.BlockSpec((features, rank), fixed),
                pl.BlockSpec((rank, rank), fixed),
                pl.BlockSpec((tile, rank), along),
                pl.BlockSpec((tile, rank), early),
                pl.BlockSpec((tile, rank), early),
                pl.BlockSpec((tile, rank), late),
                pl.BlockSpec((tile, rank), late),
            ],
            out_specs=[
                pl.BlockSpec((features, tile), column),
                pl.BlockSpec((features, rank), fixed),
                pl.BlockSpec((tile, rank), early),
                pl.BlockSpec((tile, rank), early),
            ],
            scratch_shapes=[
                pltpu.VMEM((features, rank), BF16),
                pltpu.VMEM((features, rank), BF16),
                pltpu.VMEM((tile, rank), F32),
                pltpu.VMEM((tile, rank), F32),
            ],
        ),
        compiler_params=pltpu.CompilerParams(vmem_limit_bytes=WHOLE_VMEM),
    )(where, power, mix, q_all, moment_first, moment_second, first_all, second_all)


def solution(mesh):
    placed = (P("dp", "shard"), P("dp", None), P("shard", None), P("shard", None), P("shard", None))
    return jax.shard_map(
        functools.partial(body, mesh.shape["dp"], mesh.shape["shard"]),
        mesh=mesh,
        in_specs=placed,
        out_specs=(P("shard", None), P("shard", None), P("shard", None), P("shard", None)),
        check_vma=False,
    )
```

```python
import functools
import math

import jax
import jax.numpy as jnp
from jax import lax
from jax.experimental import pallas as pl
from jax.experimental.pallas import tpu as pltpu
from jax.sharding import PartitionSpec as P

NS_STEPS = 5
F32 = jnp.float32
BF16 = jnp.bfloat16
TILE = 256
ORDER = ("line", "plane", "plane", "plane")
BLOCKS = len(ORDER)
GREET = "plane"
WHOLE_VMEM = 62 * 2**20


def split(x):
    hi = x.astype(BF16)
    return hi, (x - hi.astype(F32)).astype(BF16)


def dot(a, b, dims=((1,), (0,))):
    return lax.dot_general(a, b, (dims, ((), ())), preferred_element_type=F32)


def dot3(a, b, dims=((1,), (0,))):
    a_hi, a_lo = split(a)
    b_hi, b_lo = split(b)
    return dot(a_hi, b_hi, dims) + (dot(a_hi, b_lo, dims) + dot(a_lo, b_hi, dims))


def stages(replicas, kind):
    pairs, stride, left = [], 1, replicas
    while left % 2 == 0 and len(pairs) < 2:
        pairs.append((stride, 2))
        stride, left = stride * 2, left // 2
    line = [(stride, left)]
    if kind == "plane":
        return [(1, stride)] + line
    if kind == "line":
        return line + [(1, stride)]
    if kind == "yx":
        return pairs[::-1] + line
    if kind == "zxy":
        return line + pairs
    return pairs + line


def reduce_kernel(
    replicas, shards, pieces, blocks,
    acts_in, cot_in, basis_in, first, second,
    power, mix, q_all, first_all, second_all,
    acts, cot, basis, cot_t, acts_t, part, image, received, tok, tok_recv, gram, gram_recv, ns_g, ns_t,
    load_sem, dp_send, dp_recv, sh_send, sh_recv, fwd_send, fwd_recv,
):
    me = lax.axis_index("dp")
    own = lax.axis_index("shard")
    tokens, features = acts.shape
    rows = cot.shape[1] // shards
    rank = basis.shape[1]
    width = rank // pieces
    inverse = 1.0 / math.sqrt(tokens * replicas)
    mesh_id = pl.DeviceIdType.MESH

    loads = [
        pltpu.make_async_copy(basis_in, basis, load_sem.at[0]),
        pltpu.make_async_copy(acts_in, acts, load_sem.at[1]),
        pltpu.make_async_copy(cot_in, cot, load_sem.at[2]),
    ]
    for load in loads:
        load.start()

    def place(stride, size):
        return lax.rem(lax.div(me, stride), size)

    def peer(stride, size, k):
        at = place(stride, size)
        return me + (lax.rem(at + k, size) - at) * stride

    def remote(src, dst, send, recv, where):
        copy = pltpu.make_async_remote_copy(
            src_ref=src, dst_ref=dst, send_sem=send, recv_sem=recv,
            device_id=where, device_id_type=mesh_id,
        )
        copy.start()
        return copy

    def to_shard(k):
        return (me, lax.rem(own + k, shards))

    barrier = pltpu.get_barrier_semaphore()
    greeted = 0
    for stride, size in stages(replicas, GREET):
        for k in range(1, size):
            pl.semaphore_signal(barrier, inc=1, device_id=(peer(stride, size, k), own), device_id_type=mesh_id)
            greeted += 1
    for k in range(1, shards):
        pl.semaphore_signal(barrier, inc=1, device_id=to_shard(k), device_id_type=mesh_id)
        greeted += 1

    def tiles(start, count, fn):
        step = min(TILE, count)
        if count == step:
            fn(start, step)
            return

        def one(i, carry):
            fn(pl.multiple_of(start + i * step, step), step)
            return carry

        lax.fori_loop(0, count // step, one, 0)

    def turn_cot(at, n):
        cot_t[pl.ds(at, n), :] = cot[:, pl.ds(pl.multiple_of(own * rows + at, 128), n)].T

    def turn_acts(at, n):
        acts_t[pl.ds(at, n), :] = acts[:, pl.ds(at, n)].T

    def read(ref, count, at, n):
        if pieces == 1:
            return ref[pl.ds(at, n), :]
        return jnp.concatenate([ref[pl.ds(s * count + at, n), :] for s in range(pieces)], axis=1)

    def contract(left, column, hi, lo, at, n, out, fresh):
        block = left[:, pl.ds(pl.multiple_of(column + at, 128), n)]
        value = dot(block, hi) + dot(block, lo)
        if fresh:
            out[...] = value
        else:
            out[...] += value

    def exchange(index, buffer, target):
        return [
            remote(buffer, target.at[k - 1], sh_send.at[index, k - 1], sh_recv.at[index, k - 1], to_shard(k))
            for k in range(1, shards)
        ]

    def total(copies, buffer, arrived):
        value = buffer[...]
        for k, copy in enumerate(copies):
            copy.wait()
            value = value + arrived[k]
        return value

    def piece(index, h, count, left, hi, lo, full, consume):
        length = count * pieces // blocks
        base = h * length

        def expand(at, n):
            block = left[pl.ds(at, n), :]
            value = dot(block, hi) + dot(block, lo)
            for s in range(pieces):
                part[pl.ds(s * count + at, n), :] = value[:, s * width : (s + 1) * width]

        tiles(h * (count // blocks), count // blocks, expand)
        slot = index * blocks + h
        path = stages(replicas, ORDER[h])
        store = slot * length
        for stage, (stride, size) in enumerate(path):
            chunk = length // size
            at = place(stride, size)
            here = store
            copies = [
                remote(
                    part.at[pl.ds(pl.multiple_of(base + lax.rem(at + k, size) * chunk, 8), chunk), :],
                    received.at[pl.ds(here + (k - 1) * chunk, chunk), :],
                    dp_send.at[slot, stage, k - 1], dp_recv.at[slot, stage, k - 1], (peer(stride, size, k), own),
                )
                for k in range(1, size)
            ]
            yield
            base = pl.multiple_of(base + at * chunk, 8)
            length = chunk
            value = part[pl.ds(base, chunk), :]
            for k, copy in enumerate(copies):
                copy.wait()
                value = value + received[pl.ds(here + k * chunk, chunk), :]
            store = store + (size - 1) * chunk
            if stage + 1 < len(path):
                part[pl.ds(base, chunk), :] = value
            else:
                full[pl.ds(base, chunk), :] = value
        for stage, (stride, size) in reversed(list(enumerate(path))):
            mine = full.at[pl.ds(base, length), :]
            copies = [
                remote(
                    mine, mine,
                    dp_send.at[slot, 3 + stage, k - 1], dp_recv.at[slot, 3 + stage, k - 1], (peer(stride, size, k), own),
                )
                for k in range(1, size)
            ]
            yield
            for copy in copies:
                copy.wait()
            base = pl.multiple_of(base - place(stride, size) * length, 8)
            length = length * size
        consume(h)

    def run(index, count, left, value, full, consume, beside=None):
        hi, lo = split(value)
        active = []
        for h in range(blocks):
            active.append(piece(index, h, count, left, hi, lo, full, consume))
            next(active[h])
        if beside is not None:
            active.append(beside())
        while active:
            active = [one for one in active if next(one, one) is None]

    loads[0].wait()
    loads[1].wait()

    def project(at, n):
        hi, lo = split(basis[pl.ds(at, n), :])
        block = acts[:, pl.ds(at, n)]
        tok[0] += dot(block, hi) + dot(block, lo)

    tok[0] = jnp.zeros_like(tok[0])
    tiles(0, features, project)
    loads[2].wait()
    pl.semaphore_wait(barrier, greeted)
    copies = exchange(0, tok.at[0], tok_recv.at[0])
    tiles(0, rows, turn_cot)
    value = total(copies, tok.at[0], tok_recv.at[0]) * inverse
    moments = []

    def early():
        for k in range(1, shards):
            slot = pl.ds((shards - k - 1) * rows, rows)
            moments.append(remote(
                first, first_all.at[slot, :], sh_send.at[4, k - 1], sh_recv.at[4, k - 1], to_shard(k)))
            moments.append(remote(
                second, second_all.at[slot, :], sh_send.at[5, k - 1], sh_recv.at[5, k - 1], to_shard(k)))
        tiles(0, features, turn_acts)
        yield

    def use_image(h):
        def one(at, n):
            hi, lo = split(read(image, rows, at, n))
            contract(cot, own * rows, hi, lo, at, n, tok.at[1], h == 0)

        tiles(h * (rows // blocks), rows // blocks, one)

    run(0, rows, cot_t, value, image, use_image, early)
    copies = exchange(1, tok.at[1], tok_recv.at[1])
    value = total(copies, tok.at[1], tok_recv.at[1]) * inverse

    def use_power(h):
        def one(at, n):
            hi, lo = split(read(power, features, at, n))
            contract(acts, 0, hi, lo, at, n, tok.at[2], h == 0)
            hi_t = hi.T
            cross = dot(hi_t, lo)
            value = dot(hi_t, hi) + (cross + cross.T)
            if h == 0:
                gram[...] = value
            else:
                gram[...] += value

        tiles(h * (features // blocks), features // blocks, one)

    run(1, features, acts_t, value, power, use_power)
    copies = exchange(2, tok.at[2], tok_recv.at[2])
    gram_copies = exchange(3, gram, gram_recv)
    value = total(copies, tok.at[2], tok_recv.at[2]) * inverse

    def newton():
        g = total(gram_copies, gram, gram_recv)
        diagonal = lax.broadcasted_iota(jnp.int32, g.shape, 0) == lax.broadcasted_iota(jnp.int32, g.shape, 1)
        scale = jnp.sqrt(jnp.sum(jnp.where(diagonal, g, 0.0), keepdims=True))
        g = g / (scale * scale)

        def factor_of(g):
            return jnp.where(diagonal, 1.5, 0.0) - 0.5 * g

        ns_g[...] = g
        ns_t[...] = factor_of(g)
        yield
        for _ in range(NS_STEPS - 1):
            factor = factor_of(ns_g[...])
            g = dot3(dot3(ns_g[...], factor), factor)
            ns_g[...] = g
            ns_t[...] = dot3(ns_t[...], factor_of(g))
            yield
        mix[...] = ns_t[...] / scale

    forwards = []

    def pass_on(h):
        n = rows * pieces // blocks
        at = h * n
        for k in range(1, shards):
            forwards.append(remote(
                q_all.at[pl.ds(at, n), :],
                q_all.at[pl.ds((shards - k) * rows * pieces + at, n), :],
                fwd_send.at[h, k - 1], fwd_recv.at[h, k - 1], to_shard(k),
            ))

    run(2, rows, cot_t, value, q_all, pass_on, newton)
    for copy in moments + forwards:
        copy.wait()


def finish_kernel(
    blocks, where, power, mix, q, first, second, first_far, second_far,
    step_out, basis_out, first_out, second_out, basis_hi, basis_lo, mean, square,
):
    j = pl.program_id(0)
    count = power.shape[0]
    tile = min(TILE, count)

    @pl.when(j == 0)
    def _():
        for i in range(count // tile):
            at = pl.ds(i * tile, tile)
            value = dot3(power[at, :], mix[...])
            basis_out[at, :] = value
            hi, lo = split(value)
            basis_hi[at, :] = hi
            basis_lo[at, :] = lo

    projected = dot3(q[...], mix[...])

    def adam(first, second):
        mean[...] = 0.9 * first[...] + 0.1 * projected
        square[...] = 0.999 * second[...] + 0.001 * projected * projected

    @pl.when(j < blocks)
    def _():
        adam(first, second)
        first_out[...] = mean[...]
        second_out[...] = square[...]

    @pl.when(j >= blocks)
    def _():
        adam(first_far, second_far)

    direction = mean[...] / (1.0 - 0.9**10) / (jnp.sqrt(square[...] / (1.0 - 0.999**10)) + 1e-08)
    hi, lo = split(direction)
    hi, lo = hi.T, lo.T
    for i in range(count // tile):
        at = pl.ds(i * tile, tile)
        a_hi = basis_hi[at, :]
        step_out[at, :] = dot(a_hi, hi) + (dot(a_hi, lo) + dot(basis_lo[at, :], hi))


def body(replicas, shards, acts, cotangents, basis_old, moment_first, moment_second):
    tokens, features = acts.shape
    outs = cotangents.shape[1]
    rows = outs // shards
    rank = basis_old.shape[1]
    least = min(rows, features)
    pieces = 1 if least // replicas % 8 == 0 else 2
    blocks = BLOCKS
    while blocks > 1 and least * pieces // (replicas * blocks) % 8:
        blocks //= 2
    width = rank // pieces
    most = max(rows, features) * pieces
    vmem = pl.BlockSpec(memory_space=pltpu.VMEM)
    hbm = pl.BlockSpec(memory_space=pltpu.HBM)
    links = max(size for _, size in stages(replicas, "plane"))
    slots = 3 * blocks
    sem = pltpu.SemaphoreType.DMA
    far = (max(shards - 1, 1) * rows, rank)
    power, mix, q_all, first_all, second_all = pl.pallas_call(
        functools.partial(reduce_kernel, replicas, shards, pieces, blocks),
        out_shape=[
            jax.ShapeDtypeStruct((features * pieces, width), F32),
            jax.ShapeDtypeStruct((rank, rank), F32),
            jax.ShapeDtypeStruct((outs * pieces, width), F32),
            jax.ShapeDtypeStruct(far, F32),
            jax.ShapeDtypeStruct(far, F32),
        ],
        in_specs=[hbm] * 5,
        out_specs=[vmem] * 3 + [hbm] * 2,
        scratch_shapes=[
            pltpu.VMEM((tokens, features), BF16),
            pltpu.VMEM((tokens, outs), BF16),
            pltpu.VMEM((features, rank), F32),
            pltpu.VMEM((rows, tokens), BF16),
            pltpu.VMEM((features, tokens), BF16),
            pltpu.VMEM((most, width), F32),
            pltpu.VMEM((rows * pieces, width), F32),
            pltpu.VMEM((3 * most, width), F32),
            pltpu.VMEM((3, tokens, rank), F32),
            pltpu.VMEM((3, shards - 1, tokens, rank), F32),
            pltpu.VMEM((rank, rank), F32),
            pltpu.VMEM((shards - 1, rank, rank), F32),
            pltpu.VMEM((rank, rank), F32),
            pltpu.VMEM((rank, rank), F32),
            sem((3,)),
            sem((slots, 6, links)),
            sem((slots, 6, links)),
            sem((6, shards)),
            sem((6, shards)),
            sem((blocks, shards)),
            sem((blocks, shards)),
        ],
        compiler_params=pltpu.CompilerParams(
            collective_id=0, has_side_effects=True, vmem_limit_bytes=WHOLE_VMEM
        ),
    )(acts, cotangents, basis_old, moment_first, moment_second)
    if pieces > 1:
        power = power.reshape(pieces, features, width).transpose(1, 0, 2).reshape(features, rank)
        q_all = q_all.reshape(shards, pieces, rows, width).transpose(0, 2, 1, 3).reshape(outs, rank)

    tile = min(TILE, rows)
    blocks = rows // tile
    where = lax.axis_index("shard").astype(jnp.int32).reshape(1)

    def column(j, at):
        return (0, lax.rem(at[0] + lax.div(j, blocks), shards) * blocks + lax.rem(j, blocks))

    fixed = lambda j, at: (0, 0)
    along = lambda j, at: (j, 0)
    early = lambda j, at: (jnp.minimum(j, blocks - 1), 0)
    late = lambda j, at: (jnp.maximum(j - blocks, 0), 0)
    return pl.pallas_call(
        functools.partial(finish_kernel, blocks),
        out_shape=[
            jax.ShapeDtypeStruct((features, outs), F32),
            jax.ShapeDtypeStruct((features, rank), F32),
            jax.ShapeDtypeStruct((rows, rank), F32),
            jax.ShapeDtypeStruct((rows, rank), F32),
        ],
        grid_spec=pltpu.PrefetchScalarGridSpec(
            num_scalar_prefetch=1,
            grid=(outs // tile,),
            in_specs=[
                pl.BlockSpec((features, rank), fixed),
                pl.BlockSpec((rank, rank), fixed),
                pl.BlockSpec((tile, rank), along),
                pl.BlockSpec((tile, rank), early),
                pl.BlockSpec((tile, rank), early),
                pl.BlockSpec((tile, rank), late),
                pl.BlockSpec((tile, rank), late),
            ],
            out_specs=[
                pl.BlockSpec((features, tile), column),
                pl.BlockSpec((features, rank), fixed),
                pl.BlockSpec((tile, rank), early),
                pl.BlockSpec((tile, rank), early),
            ],
            scratch_shapes=[
                pltpu.VMEM((features, rank), BF16),
                pltpu.VMEM((features, rank), BF16),
                pltpu.VMEM((tile, rank), F32),
                pltpu.VMEM((tile, rank), F32),
            ],
        ),
        compiler_params=pltpu.CompilerParams(vmem_limit_bytes=WHOLE_VMEM),
    )(where, power, mix, q_all, moment_first, moment_second, first_all, second_all)


def solution(mesh):
    placed = (P("dp", "shard"), P("dp", None), P("shard", None), P("shard", None), P("shard", None))
    return jax.shard_map(
        functools.partial(body, mesh.shape["dp"], mesh.shape["shard"]),
        mesh=mesh,
        in_specs=placed,
        out_specs=(P("shard", None), P("shard", None), P("shard", None), P("shard", None)),
        check_vma=False,
    )
```

```python
import functools
import math

import jax
import jax.numpy as jnp
from jax import lax
from jax.experimental import pallas as pl
from jax.experimental.pallas import tpu as pltpu
from jax.sharding import PartitionSpec as P

NS_STEPS = 5
F32 = jnp.float32
BF16 = jnp.bfloat16
TILE = 256
ORDER = ("line", "plane", "plane", "plane")
BLOCKS = len(ORDER)
GREET = "plane"
WHOLE_VMEM = 62 * 2**20


def split(x):
    hi = x.astype(BF16)
    return hi, (x - hi.astype(F32)).astype(BF16)


def dot(a, b, dims=((1,), (0,))):
    return lax.dot_general(a, b, (dims, ((), ())), preferred_element_type=F32)


def dot3(a, b, dims=((1,), (0,))):
    a_hi, a_lo = split(a)
    b_hi, b_lo = split(b)
    return dot(a_hi, b_hi, dims) + (dot(a_hi, b_lo, dims) + dot(a_lo, b_hi, dims))


def stages(replicas, kind):
    pairs, stride, left = [], 1, replicas
    while left % 2 == 0 and len(pairs) < 2:
        pairs.append((stride, 2))
        stride, left = stride * 2, left // 2
    line = [(stride, left)]
    if kind == "plane":
        return [(1, stride)] + line
    if kind == "line":
        return line + [(1, stride)]
    if kind == "yx":
        return pairs[::-1] + line
    if kind == "zxy":
        return line + pairs
    return pairs + line


def reduce_kernel(
    replicas, shards, pieces, blocks,
    acts_in, cot_in, basis_in, first, second,
    power, mix, q_all, first_all, second_all,
    acts, cot, basis, cot_t, acts_t, part, image, received, tok, tok_recv, gram, gram_recv, ns_g, ns_t,
    load_sem, dp_send, dp_recv, sh_send, sh_recv, fwd_send, fwd_recv,
):
    me = lax.axis_index("dp")
    own = lax.axis_index("shard")
    tokens, features = acts.shape
    rows = cot.shape[1] // shards
    rank = basis.shape[1]
    width = rank // pieces
    inverse = 1.0 / math.sqrt(tokens * replicas)
    mesh_id = pl.DeviceIdType.MESH

    loads = [
        pltpu.make_async_copy(basis_in, basis, load_sem.at[0]),
        pltpu.make_async_copy(acts_in, acts, load_sem.at[1]),
        pltpu.make_async_copy(cot_in, cot, load_sem.at[2]),
    ]
    for load in loads:
        load.start()

    def place(stride, size):
        return lax.rem(lax.div(me, stride), size)

    def peer(stride, size, k):
        at = place(stride, size)
        return me + (lax.rem(at + k, size) - at) * stride

    def remote(src, dst, send, recv, where):
        copy = pltpu.make_async_remote_copy(
            src_ref=src, dst_ref=dst, send_sem=send, recv_sem=recv,
            device_id=where, device_id_type=mesh_id,
        )
        copy.start()
        return copy

    def to_shard(k):
        return (me, lax.rem(own + k, shards))

    barrier = pltpu.get_barrier_semaphore()
    greeted = 0
    for stride, size in stages(replicas, GREET):
        for k in range(1, size):
            pl.semaphore_signal(barrier, inc=1, device_id=(peer(stride, size, k), own), device_id_type=mesh_id)
            greeted += 1
    for k in range(1, shards):
        pl.semaphore_signal(barrier, inc=1, device_id=to_shard(k), device_id_type=mesh_id)
        greeted += 1

    def tiles(start, count, fn):
        step = min(TILE, count)
        if count == step:
            fn(start, step)
            return

        def one(i, carry):
            fn(pl.multiple_of(start + i * step, step), step)
            return carry

        lax.fori_loop(0, count // step, one, 0)

    def turn_cot(at, n):
        cot_t[pl.ds(at, n), :] = cot[:, pl.ds(pl.multiple_of(own * rows + at, 128), n)].T

    def turn_acts(at, n):
        acts_t[pl.ds(at, n), :] = acts[:, pl.ds(at, n)].T

    def read(ref, count, at, n):
        if pieces == 1:
            return ref[pl.ds(at, n), :]
        return jnp.concatenate([ref[pl.ds(s * count + at, n), :] for s in range(pieces)], axis=1)

    def contract(left, column, hi, lo, at, n, out, fresh):
        block = left[:, pl.ds(pl.multiple_of(column + at, 128), n)]
        value = dot(block, hi) + dot(block, lo)
        if fresh:
            out[...] = value
        else:
            out[...] += value

    def exchange(index, buffer, target):
        return [
            remote(buffer, target.at[k - 1], sh_send.at[index, k - 1], sh_recv.at[index, k - 1], to_shard(k))
            for k in range(1, shards)
        ]

    def total(copies, buffer, arrived):
        value = buffer[...]
        for k, copy in enumerate(copies):
            copy.wait()
            value = value + arrived[k]
        return value

    def piece(index, h, count, left, hi, lo, full, consume):
        length = count * pieces // blocks
        base = h * length

        def expand(at, n):
            block = left[pl.ds(at, n), :]
            value = dot(block, hi) + dot(block, lo)
            for s in range(pieces):
                part[pl.ds(s * count + at, n), :] = value[:, s * width : (s + 1) * width]

        tiles(h * (count // blocks), count // blocks, expand)
        slot = index * blocks + h
        path = stages(replicas, ORDER[h])
        store = slot * length
        for stage, (stride, size) in enumerate(path):
            chunk = length // size
            at = place(stride, size)
            here = store
            copies = [
                remote(
                    part.at[pl.ds(pl.multiple_of(base + lax.rem(at + k, size) * chunk, 8), chunk), :],
                    received.at[pl.ds(here + (k - 1) * chunk, chunk), :],
                    dp_send.at[slot, stage, k - 1], dp_recv.at[slot, stage, k - 1], (peer(stride, size, k), own),
                )
                for k in range(1, size)
            ]
            yield
            base = pl.multiple_of(base + at * chunk, 8)
            length = chunk
            value = part[pl.ds(base, chunk), :]
            for k, copy in enumerate(copies):
                copy.wait()
                value = value + received[pl.ds(here + k * chunk, chunk), :]
            store = store + (size - 1) * chunk
            if stage + 1 < len(path):
                part[pl.ds(base, chunk), :] = value
            else:
                full[pl.ds(base, chunk), :] = value
        for stage, (stride, size) in reversed(list(enumerate(path))):
            mine = full.at[pl.ds(base, length), :]
            copies = [
                remote(
                    mine, mine,
                    dp_send.at[slot, 3 + stage, k - 1], dp_recv.at[slot, 3 + stage, k - 1], (peer(stride, size, k), own),
                )
                for k in range(1, size)
            ]
            yield
            for copy in copies:
                copy.wait()
            base = pl.multiple_of(base - place(stride, size) * length, 8)
            length = length * size
        consume(h)

    def run(index, count, left, value, full, consume, beside=None):
        hi, lo = split(value)
        active = []
        for h in range(blocks):
            active.append(piece(index, h, count, left, hi, lo, full, consume))
            next(active[h])
        if beside is not None:
            active.append(beside())
        while active:
            active = [one for one in active if next(one, one) is None]

    loads[0].wait()
    loads[1].wait()

    def project(at, n):
        hi, lo = split(basis[pl.ds(at, n), :])
        block = acts[:, pl.ds(at, n)]
        tok[0] += dot(block, hi) + dot(block, lo)

    tok[0] = jnp.zeros_like(tok[0])
    tiles(0, features, project)
    loads[2].wait()
    pl.semaphore_wait(barrier, greeted)
    copies = exchange(0, tok.at[0], tok_recv.at[0])
    tiles(0, rows, turn_cot)
    value = total(copies, tok.at[0], tok_recv.at[0]) * inverse
    moments = []

    def early():
        for k in range(1, shards):
            slot = pl.ds((shards - k - 1) * rows, rows)
            moments.append(remote(
                first, first_all.at[slot, :], sh_send.at[4, k - 1], sh_recv.at[4, k - 1], to_shard(k)))
            moments.append(remote(
                second, second_all.at[slot, :], sh_send.at[5, k - 1], sh_recv.at[5, k - 1], to_shard(k)))
        tiles(0, features, turn_acts)
        yield

    def use_image(h):
        def one(at, n):
            hi, lo = split(read(image, rows, at, n))
            contract(cot, own * rows, hi, lo, at, n, tok.at[1], h == 0)

        tiles(h * (rows // blocks), rows // blocks, one)

    run(0, rows, cot_t, value, image, use_image, early)
    copies = exchange(1, tok.at[1], tok_recv.at[1])
    value = total(copies, tok.at[1], tok_recv.at[1]) * inverse

    def use_power(h):
        def one(at, n):
            hi, lo = split(read(power, features, at, n))
            contract(acts, 0, hi, lo, at, n, tok.at[2], h == 0)
            hi_t = hi.T
            cross = dot(hi_t, lo)
            value = dot(hi_t, hi) + (cross + cross.T)
            if h == 0:
                gram[...] = value
            else:
                gram[...] += value

        tiles(h * (features // blocks), features // blocks, one)

    run(1, features, acts_t, value, power, use_power)
    copies = exchange(2, tok.at[2], tok_recv.at[2])
    gram_copies = exchange(3, gram, gram_recv)
    value = total(copies, tok.at[2], tok_recv.at[2]) * inverse

    def newton():
        g = total(gram_copies, gram, gram_recv)
        diagonal = lax.broadcasted_iota(jnp.int32, g.shape, 0) == lax.broadcasted_iota(jnp.int32, g.shape, 1)
        scale = jnp.sqrt(jnp.sum(jnp.where(diagonal, g, 0.0), keepdims=True))
        g = g / (scale * scale)

        def factor_of(g):
            return jnp.where(diagonal, 1.5, 0.0) - 0.5 * g

        ns_g[...] = g
        ns_t[...] = factor_of(g)
        yield
        for _ in range(NS_STEPS - 1):
            factor = factor_of(ns_g[...])
            g = dot3(dot3(ns_g[...], factor), factor)
            ns_g[...] = g
            ns_t[...] = dot3(ns_t[...], factor_of(g))
            yield
        mix[...] = ns_t[...] / scale

    forwards = []

    def pass_on(h):
        n = rows * pieces // blocks
        at = h * n
        for k in range(1, shards):
            forwards.append(remote(
                q_all.at[pl.ds(at, n), :],
                q_all.at[pl.ds((shards - k) * rows * pieces + at, n), :],
                fwd_send.at[h, k - 1], fwd_recv.at[h, k - 1], to_shard(k),
            ))

    run(2, rows, cot_t, value, q_all, pass_on, newton)
    for copy in moments + forwards:
        copy.wait()


def finish_kernel(
    blocks, where, power, mix, q, first, second, first_far, second_far,
    step_out, basis_out, first_out, second_out, basis_hi, basis_lo, mean, square,
):
    j = pl.program_id(0)
    count = power.shape[0]
    tile = min(TILE, count)

    @pl.when(j == 0)
    def _():
        for i in range(count // tile):
            at = pl.ds(i * tile, tile)
            value = dot3(power[at, :], mix[...])
            basis_out[at, :] = value
            hi, lo = split(value)
            basis_hi[at, :] = hi
            basis_lo[at, :] = lo

    projected = dot3(q[...], mix[...])

    def adam(first, second):
        mean[...] = 0.9 * first[...] + 0.1 * projected
        square[...] = 0.999 * second[...] + 0.001 * projected * projected

    @pl.when(j < blocks)
    def _():
        adam(first, second)
        first_out[...] = mean[...]
        second_out[...] = square[...]

    @pl.when(j >= blocks)
    def _():
        adam(first_far, second_far)

    direction = mean[...] / (1.0 - 0.9**10) / (jnp.sqrt(square[...] / (1.0 - 0.999**10)) + 1e-08)
    hi, lo = split(direction)
    hi, lo = hi.T, lo.T
    for i in range(count // tile):
        at = pl.ds(i * tile, tile)
        a_hi = basis_hi[at, :]
        step_out[at, :] = dot(a_hi, hi) + (dot(a_hi, lo) + dot(basis_lo[at, :], hi))


def body(replicas, shards, acts, cotangents, basis_old, moment_first, moment_second):
    tokens, features = acts.shape
    outs = cotangents.shape[1]
    rows = outs // shards
    rank = basis_old.shape[1]
    least = min(rows, features)
    pieces = 1 if least // replicas % 8 == 0 else 2
    blocks = BLOCKS
    while blocks > 1 and least * pieces // (replicas * blocks) % 8:
        blocks //= 2
    width = rank // pieces
    most = max(rows, features) * pieces
    vmem = pl.BlockSpec(memory_space=pltpu.VMEM)
    hbm = pl.BlockSpec(memory_space=pltpu.HBM)
    links = max(size for _, size in stages(replicas, "plane"))
    slots = 3 * blocks
    sem = pltpu.SemaphoreType.DMA
    far = (max(shards - 1, 1) * rows, rank)
    power, mix, q_all, first_all, second_all = pl.pallas_call(
        functools.partial(reduce_kernel, replicas, shards, pieces, blocks),
        out_shape=[
            jax.ShapeDtypeStruct((features * pieces, width), F32),
            jax.ShapeDtypeStruct((rank, rank), F32),
            jax.ShapeDtypeStruct((outs * pieces, width), F32),
            jax.ShapeDtypeStruct(far, F32),
            jax.ShapeDtypeStruct(far, F32),
        ],
        in_specs=[hbm] * 5,
        out_specs=[vmem] * 3 + [hbm] * 2,
        scratch_shapes=[
            pltpu.VMEM((tokens, features), BF16),
            pltpu.VMEM((tokens, outs), BF16),
            pltpu.VMEM((features, rank), F32),
            pltpu.VMEM((rows, tokens), BF16),
            pltpu.VMEM((features, tokens), BF16),
            pltpu.VMEM((most, width), F32),
            pltpu.VMEM((rows * pieces, width), F32),
            pltpu.VMEM((3 * most, width), F32),
            pltpu.VMEM((3, tokens, rank), F32),
            pltpu.VMEM((3, shards - 1, tokens, rank), F32),
            pltpu.VMEM((rank, rank), F32),
            pltpu.VMEM((shards - 1, rank, rank), F32),
            pltpu.VMEM((rank, rank), F32),
            pltpu.VMEM((rank, rank), F32),
            sem((3,)),
            sem((slots, 6, links)),
            sem((slots, 6, links)),
            sem((6, shards)),
            sem((6, shards)),
            sem((blocks, shards)),
            sem((blocks, shards)),
        ],
        compiler_params=pltpu.CompilerParams(
            collective_id=0, has_side_effects=True, vmem_limit_bytes=WHOLE_VMEM
        ),
    )(acts, cotangents, basis_old, moment_first, moment_second)
    if pieces > 1:
        power = power.reshape(pieces, features, width).transpose(1, 0, 2).reshape(features, rank)
        q_all = q_all.reshape(shards, pieces, rows, width).transpose(0, 2, 1, 3).reshape(outs, rank)

    tile = min(2 * TILE, rows)
    blocks = rows // tile
    where = lax.axis_index("shard").astype(jnp.int32).reshape(1)

    def column(j, at):
        return (0, lax.rem(at[0] + lax.div(j, blocks), shards) * blocks + lax.rem(j, blocks))

    fixed = lambda j, at: (0, 0)
    along = lambda j, at: (j, 0)
    early = lambda j, at: (jnp.minimum(j, blocks - 1), 0)
    late = lambda j, at: (jnp.maximum(j - blocks, 0), 0)
    return pl.pallas_call(
        functools.partial(finish_kernel, blocks),
        out_shape=[
            jax.ShapeDtypeStruct((features, outs), F32),
            jax.ShapeDtypeStruct((features, rank), F32),
            jax.ShapeDtypeStruct((rows, rank), F32),
            jax.ShapeDtypeStruct((rows, rank), F32),
        ],
        grid_spec=pltpu.PrefetchScalarGridSpec(
            num_scalar_prefetch=1,
            grid=(outs // tile,),
            in_specs=[
                pl.BlockSpec((features, rank), fixed),
                pl.BlockSpec((rank, rank), fixed),
                pl.BlockSpec((tile, rank), along),
                pl.BlockSpec((tile, rank), early),
                pl.BlockSpec((tile, rank), early),
                pl.BlockSpec((tile, rank), late),
                pl.BlockSpec((tile, rank), late),
            ],
            out_specs=[
                pl.BlockSpec((features, tile), column),
                pl.BlockSpec((features, rank), fixed),
                pl.BlockSpec((tile, rank), early),
                pl.BlockSpec((tile, rank), early),
            ],
            scratch_shapes=[
                pltpu.VMEM((features, rank), BF16),
                pltpu.VMEM((features, rank), BF16),
                pltpu.VMEM((tile, rank), F32),
                pltpu.VMEM((tile, rank), F32),
            ],
        ),
        compiler_params=pltpu.CompilerParams(vmem_limit_bytes=WHOLE_VMEM),
    )(where, power, mix, q_all, moment_first, moment_second, first_all, second_all)


def solution(mesh):
    placed = (P("dp", "shard"), P("dp", None), P("shard", None), P("shard", None), P("shard", None))
    return jax.shard_map(
        functools.partial(body, mesh.shape["dp"], mesh.shape["shard"]),
        mesh=mesh,
        in_specs=placed,
        out_specs=(P("shard", None), P("shard", None), P("shard", None), P("shard", None)),
        check_vma=False,
    )
```
